32 devices in a mesh: groups: 2 (over y), mp: 4 (over z), dp: 2 (over x), guide: 2 (over core).
Axes of the slice: x: 2, y: 2, z: 4, core: 2. Of those that a mesh axis runs over, the one named last changes fastest.
Arguments:
- tokens: bfloat16 [192, 8192], P(('groups', 'mp'), ('dp', 'guide')), parts along dimension 0, may hold values from -6 to 6
- w_gate: bfloat16 [8192, 14336], P(('dp', 'guide'), 'mp'), may hold values from -0.0625 to 0.0625
- w_up: bfloat16 [8192, 14336], P(('dp', 'guide'), 'mp'), may hold values from -0.0625 to 0.0625
- w_down: bfloat16 [14336, 8192], P('mp', ('dp', 'guide')), may hold values from -0.046875 to 0.046875
Outputs:
- layer_output: bfloat16 [192, 8192], P(('groups', 'mp'), ('dp', 'guide')), parts along dimension 0
The draws below stay inside these ranges and needn't reach their ends.
There are 2 independent parts, one for each index of `groups`. The reference program is written for one: setup_inputs(seed, part) draws one part's arguments, and reference() takes and returns one part's arrays. A program takes and returns all parts, laid end to end along the dimension named above; an argument that names none is the same for every part. Nothing has to cross between parts.
All inputs are finite; a program needn't handle non-finite values.
Results may differ from the reference program's by a relative error of at most 0.0049.
Values may be sent and summed in bfloat16 or wider, within the bound.
A program may use at most 128 MiB of HBM per device.

```python
import jax
import jax.numpy as jnp

D = 8192
FF = 14336
ROWS = 96


def level_of(own_key, shape, split, least, largest):
    level, own = 1.0, jax.random.fold_in(own_key, 6)
    for dim, parts in split:
        steps = jnp.exp(jax.random.uniform(jax.random.fold_in(own, dim), (parts,), jnp.float32, least / len(split), largest / len(split)))
        level = level * jnp.repeat(steps, shape[dim] // parts).reshape([-1 if axis == dim else 1 for axis in range(len(shape))])
    return level


def gaussian(key, dims, deviation, reach, cuts=(), dtype=jnp.bfloat16):
    result = jax.random.normal(key, dims, jnp.float32) * deviation
    if len(cuts) > 0:
        result = level_of(key, dims, cuts, -0.22, 0.18) * result
    return jnp.clip(result, min=-reach, max=reach).astype(dtype)


def setup_inputs(seed: int = 0, part: int = 0) -> dict:
    splits = jax.random.split(jax.random.key(seed), 5)
    part_keys = jax.random.split(jax.random.fold_in(splits[4], part), 5)
    tokens = gaussian(part_keys[0], (ROWS, D), 1.0, 6.0, ((0, 4), (1, 4)))
    w_gate = gaussian(splits[1], (D, FF), D ** -0.5, 0.0625, ((0, 4), (1, 4)))
    w_up = gaussian(splits[2], (D, FF), D ** -0.5, 0.0625, ((0, 4), (1, 4)))
    w_down = gaussian(splits[3], (FF, D), FF ** -0.5, 0.046875, ((0, 4), (1, 4)))
    return dict(tokens=tokens, w_gate=w_gate, w_up=w_up, w_down=w_down)


def reference(tokens, w_gate, w_up, w_down):
    gate_sum = jnp.dot(tokens, w_gate, preferred_element_type=jnp.float32)
    up_sum = jnp.dot(tokens, w_up, preferred_element_type=jnp.float32)
    hidden = (jax.nn.silu(gate_sum) * up_sum).astype(jnp.bfloat16)
    total = jnp.dot(hidden, w_down, preferred_element_type=jnp.float32)
    return total.astype(jnp.bfloat16)
```

```python
import functools

import jax
import jax.numpy as jnp
from jax import lax
from jax.experimental import pallas as pl
from jax.experimental.pallas import tpu as pltpu
from jax.sharding import PartitionSpec as P

MESH = pl.DeviceIdType.MESH
F32, BF16 = jnp.float32, jnp.bfloat16
PIECES = 4
K_GROUPS = ((0, 2), (2, 3), (3, 4))
N_OUT = 4


def splits(width, most):
    cuts = list(range(0, width, most)) + [width]
    return tuple((lo, hi - lo) for lo, hi in zip(cuts, cuts[1:]))


BLOCKS = ((0, 1), (1, 2), (2, 4))


def kernel(tokens, w_gate, w_up, w_down, out, *scratch):
    (gate_v, up_v, down_v, tok_in, tok_f, tok, out_send, out_recv,
     w_sem, rest_sem, down_sem, tok_own, tok_s, tok_r, c_s, c_r) = scratch[:16]
    names = ("sum1_out", "sum1_in", "kept", "sum2_out", "sum2_in", "hid", "acc",
             "s1_s", "s1_r", "s2_s", "s2_r", "hx_s", "hx_r", "hc_s", "hc_r", "hr_s", "hr_r")
    (sum1_out, sum1_in, kept, sum2_out, sum2_in, hid, acc,
     s1_s, s1_r, s2_s, s2_r, hx_s, hx_r, hc_s, hc_r, hr_s, hr_r) = [
        [scratch[16 + len(names) * b + i] for b in range(len(BLOCKS))] for i in range(len(names))]
    m, d, g = lax.axis_index("mp"), lax.axis_index("dp"), lax.axis_index("guide")
    rows, depth = tokens.shape
    quarter = gate_v.shape[2]
    wide = down_v.shape[1]
    cols = [chunks(b, quarter) for b in range(len(BLOCKS))]
    piece = depth // PIECES
    n_width = wide // N_OUT
    z1 = m + 1 - 2 * lax.rem(m, 2)
    z2 = lax.rem(m + 2, 4)
    z3 = 3 - m
    mid = lax.rem(m + 1, 4) // 2
    to_dp, to_core = {"dp": 1 - d}, {"guide": 1 - g}

    barrier = pltpu.get_barrier_semaphore()
    for device in ({"mp": z1}, {"mp": z2}, {"mp": z3}, to_dp, to_core):
        pl.semaphore_signal(barrier, inc=1, device_id=device, device_id_type=MESH)

    def region(dd, gg):
        return pl.multiple_of((gg * 2 + dd) * quarter, 128)

    regions = (region(1 - d, 1 - g), region(1 - d, g), region(d, 1 - g), region(d, g))
    hid_regions = (region(d, g), region(d, 1 - g), region(1 - d, g), region(1 - d, 1 - g))

    def weights(kg, s):
        k = pl.ds(K_GROUPS[kg][0] * piece, (K_GROUPS[kg][1] - K_GROUPS[kg][0]) * piece)
        src = pl.ds(regions[s], quarter)
        return (pltpu.make_async_copy(w_gate.at[k, src], gate_v.at[s, k, :], w_sem.at[0, kg, s]),
                pltpu.make_async_copy(w_up.at[k, src], up_v.at[s, k, :], w_sem.at[1, kg, s]))

    def weights_whole(s):
        src = pl.ds(regions[s], quarter)
        return (pltpu.make_async_copy(w_gate.at[:, src], gate_v.at[s], rest_sem.at[0, s - 2]),
                pltpu.make_async_copy(w_up.at[:, src], up_v.at[s], rest_sem.at[1, s - 2]))

    def downs(s):
        return pltpu.make_async_copy(
            w_down.at[pl.ds(hid_regions[s], quarter), :], down_v.at[pl.ds(s * quarter, quarter), :], down_sem.at[s])

    own = pltpu.make_async_copy(tokens, tok_in.at[3], tok_own)
    own.start()
    own.wait()
    for kg in range(len(K_GROUPS)):
        for s in range(2):
            for copy in weights(kg, s):
                copy.start()
    for s in (2, 3):
        for copy in weights_whole(s):
            copy.start()
    for s in range(4):
        downs(s).start()

    pl.semaphore_wait(barrier, 5)

    def tok_copy(p, pos, src, to):
        c = pl.ds(p * piece, piece)
        return pltpu.make_async_remote_copy(
            src_ref=src.at[:, c], dst_ref=tok_in.at[pos, :, c], send_sem=tok_s.at[pos, p], recv_sem=tok_r.at[pos, p],
            device_id={"mp": to}, device_id_type=MESH)

    def tok_z3(p):
        return tok_copy(p, 1, tok_in.at[3], z3)

    def tok_z1(p):
        return tok_copy(p, 2, tok_in.at[3], z1)

    def tok_z2(p):
        return tok_copy(p, 0, tok_in.at[3], z2)

    def tok_relay(p):
        return tok_copy(p, 0, tok_in.at[1], z1)

    for p in range(PIECES):
        tok_z3(p).start()

        @pl.when(mid == 0)
        def _():
            tok_z2(p).start()

        tok_z1(p).start()

    def forward(p):
        tok_z3(p).wait_recv()

        @pl.when(mid == 1)
        def _():
            tok_relay(p).start()

    def gather(p):
        c = slice(p * piece, (p + 1) * piece)
        tok_z1(p).wait_recv()
        tok_z2(p).wait_recv()
        for q in range(4):
            tok_f[q * rows:(q + 1) * rows, :] = tok_in[q, :, c].astype(F32)
        tok[:, c] = tok_f[...].astype(BF16)

    def add_up(s, k, first):
        to = sum1_out if s % 2 == 0 else kept
        for i, held in ((0, gate_v), (1, up_v)):
            value = jnp.dot(tok[:, k], held[s, k, :], preferred_element_type=F32)
            for b, (lo, hi) in enumerate(BLOCKS):
                part = value[lo * rows:hi * rows, :]
                if first:
                    to[b][s // 2, i] = part
                else:
                    to[b][s // 2, i] += part

    def partial(kg, s):
        for copy in weights(kg, s):
            copy.wait()
        add_up(s, slice(K_GROUPS[kg][0] * piece, K_GROUPS[kg][1] * piece), kg == 0)

    def partial_whole(s):
        for copy in weights_whole(s):
            copy.wait()
        add_up(s, slice(0, depth), True)

    def s1_copy(i, b):
        return pltpu.make_async_remote_copy(
            src_ref=sum1_out[b].at[i], dst_ref=sum1_in[b].at[i], send_sem=s1_s[b].at[i], recv_sem=s1_r[b].at[i],
            device_id=to_core, device_id_type=MESH)

    def send_core(i):
        for b in range(len(BLOCKS)):
            s1_copy(i, b).start()

    def s2_copy(b, c):
        part = pl.ds(*cols[b][c])
        return pltpu.make_async_remote_copy(
            src_ref=sum2_out[b].at[:, :, part], dst_ref=sum2_in[b].at[:, :, part],
            send_sem=s2_s[b].at[c], recv_sem=s2_r[b].at[c], device_id=to_dp, device_id_type=MESH)

    def pair_sum(b, c):
        if c == 0:
            s1_copy(0, b).wait_recv()
        part = slice(cols[b][c][0], sum(cols[b][c]))
        for i in range(2):
            sum2_out[b][i, :, part] = (kept[b][0, i, :, part] + sum1_in[b][0, i, :, part]).astype(BF16)
        s2_copy(b, c).start()

    def hid_copy(b, c, src, dst, send, recv, to):
        at, width = cols[b][c]
        return pltpu.make_async_remote_copy(
            src_ref=hid[b].at[:, pl.ds(src * quarter + at, width)], dst_ref=hid[b].at[:, pl.ds(dst * quarter + at, width)],
            send_sem=send[b].at[c], recv_sem=recv[b].at[c], device_id=to, device_id_type=MESH)

    def hx_copy(b, c):
        return hid_copy(b, c, 0, 2, hx_s, hx_r, to_dp)

    def hc_copy(b, c):
        return hid_copy(b, c, 0, 1, hc_s, hc_r, to_core)

    def hr_copy(b, c):
        return hid_copy(b, c, 2, 3, hr_s, hr_r, to_core)

    def finish(b, c):
        if c == 0:
            s1_copy(1, b).wait_recv()
        part = slice(cols[b][c][0], sum(cols[b][c]))
        s2_copy(b, c).wait_recv()
        gate, up = [kept[b][1, i, :, part] + sum1_in[b][1, i, :, part] + sum2_in[b][i, :, part].astype(F32)
                    for i in range(2)]
        hid[b][:, part] = (gate / (1.0 + jnp.exp(-gate)) * up).astype(BF16)
        hx_copy(b, c).start()
        hc_copy(b, c).start()

    def relay(b, c):
        hx_copy(b, c).wait_recv()
        hr_copy(b, c).start()

    def c_copy(n, q):
        to = (z1 + mid * (z2 - z1), z3, z1)[q]
        return pltpu.make_async_remote_copy(
            src_ref=out_send.at[n, q], dst_ref=out_recv.at[n, q], send_sem=c_s.at[n, q], recv_sem=c_r.at[n, q],
            device_id={"mp": to}, device_id_type=MESH)

    def n_cols(n):
        return slice(n * n_width, (n + 1) * n_width)

    def down_first(b):
        if b == 0:
            downs(0).wait()
            downs(1).wait()
        for c in range(len(cols[b])):
            hc_copy(b, c).wait_recv()
        for n in range(N_OUT):
            acc[b][:, n_cols(n)] = jnp.dot(
                hid[b][:, :2 * quarter], down_v[:2 * quarter, n_cols(n)], preferred_element_type=F32)

    def down_second(b):
        if b == 0:
            downs(2).wait()
            downs(3).wait()
        for c in range(len(cols[b])):
            hr_copy(b, c).wait_recv()
        for n in range(N_OUT):
            acc[b][:, n_cols(n)] += jnp.dot(
                hid[b][:, 2 * quarter:], down_v[2 * quarter:, n_cols(n)], preferred_element_type=F32)
            if b == 1:
                @pl.when(mid == 1)
                def _():
                    c_copy(n, 0).wait_recv()
                    acc[1][:, n_cols(n)] += out_recv[n, 0].astype(F32)
            out_send[n, b] = acc[b][:rows, n_cols(n)].astype(BF16)
            c_copy(n, b).start()

    def final(n):
        c_copy(n, 1).wait_recv()
        c_copy(n, 2).wait_recv()
        total = acc[2][rows:, n_cols(n)] + out_recv[n, 1].astype(F32) + out_recv[n, 2].astype(F32)
        out[:, n_cols(n)] = total.astype(BF16)

    for p in range(PIECES):
        forward(p)
    gather(0)
    gather(1)
    partial(0, 0)
    partial(0, 1)
    gather(2)
    partial(1, 0)
    partial(1, 1)
    gather(3)
    partial(2, 0)
    send_core(0)
    partial(2, 1)
    pair_sum(0, 0)
    pair_sum(0, 1)
    pair_sum(1, 0)
    pair_sum(1, 1)
    partial_whole(2)
    send_core(1)
    partial_whole(3)
    pair_sum(2, 0)
    finish(0, 0)
    finish(0, 1)
    pair_sum(2, 1)
    finish(1, 0)
    finish(1, 1)
    pair_sum(2, 2)
    pair_sum(2, 3)
    down_first(0)
    relay(0, 0)
    relay(0, 1)
    finish(2, 0)
    down_first(1)
    down_second(0)
    relay(1, 0)
    relay(1, 1)
    finish(2, 1)
    finish(2, 2)
    finish(2, 3)
    down_second(1)
    relay(2, 0)
    relay(2, 1)
    down_first(2)
    relay(2, 2)
    relay(2, 3)
    down_second(2)

    @pl.when(mid == 0)
    def _():
        for n in range(N_OUT):
            c_copy(n, 0).wait_recv()
            acc[2][rows:, n_cols(n)] += out_recv[n, 0].astype(F32)

    final(0)
    final(1)
    final(2)
    final(3)

    for p in range(PIECES):
        tok_z3(p).wait_send()
        tok_z2(p).wait_send()
        tok_z1(p).wait_send()
    for b in range(len(BLOCKS)):
        s1_copy(0, b).wait_send()
        s1_copy(1, b).wait_send()
        for c in range(len(cols[b])):
            s2_copy(b, c).wait_send()
            hx_copy(b, c).wait_send()
            hc_copy(b, c).wait_send()
            hr_copy(b, c).wait_send()
    for n in range(N_OUT):
        for q in range(3):
            c_copy(n, q).wait_send()


def chunks(b, quarter):
    lanes = quarter // 128
    return splits(quarter, (lanes + 1) // 2 * 128 if b < 2 else (lanes + 3) // 4 * 128)


def fused(tokens, w_gate, w_up, w_down):
    rows, depth = tokens.shape
    columns, wide = w_gate.shape[1], w_down.shape[1]
    quarter = columns // 4
    nk, n_width = len(K_GROUPS), wide // N_OUT
    dma, vmem = pltpu.SemaphoreType.DMA, pltpu.VMEM
    shapes = [
        vmem((4, depth, quarter), BF16),
        vmem((4, depth, quarter), BF16),
        vmem((columns, wide), BF16),
        vmem((4, rows, depth), BF16),
        vmem((4 * rows, depth // PIECES), F32),
        vmem((4 * rows, depth), BF16),
        vmem((N_OUT, 3, rows, n_width), BF16),
        vmem((N_OUT, 3, rows, n_width), BF16),
        dma((2, nk, 2)), dma((2, 2)), dma((4,)), dma, dma((3, PIECES)), dma((3, PIECES)),
        dma((N_OUT, 3)), dma((N_OUT, 3)),
    ]
    for b, (lo, hi) in enumerate(BLOCKS):
        size, nc = (hi - lo) * rows, len(chunks(b, quarter))
        shapes += [vmem((2, 2, size, quarter), F32)] * 3 + [vmem((2, size, quarter), BF16)] * 2
        shapes += [vmem((size, columns), BF16), vmem((size, wide), F32)]
        shapes += [dma((2,))] * 2 + [dma((nc,))] * 8
    return pl.pallas_call(
        kernel,
        out_shape=vmem((rows, wide), BF16),
        in_specs=[pl.BlockSpec(memory_space=pltpu.HBM)] * 4,
        out_specs=pl.BlockSpec(memory_space=vmem),
        scratch_shapes=shapes,
        compiler_params=pltpu.CompilerParams(
            collective_id=0, has_side_effects=True, vmem_limit_bytes=60 << 20),
    )(tokens, w_gate, w_up, w_down)


def by_collectives(tokens, w_gate, w_up, w_down):
    columns = w_gate.shape[1]
    paired_weights = jnp.concatenate([w_gate, w_up], axis=1)
    partial_terms = jnp.dot(
        lax.all_gather(tokens, "mp", axis=0, tiled=True), paired_weights, preferred_element_type=F32)
    summed = lax.psum_scatter(partial_terms, ("dp", "guide"), scatter_dimension=0, tiled=True)
    hidden_share = (jax.nn.silu(summed[:, :columns]) * summed[:, columns:]).astype(BF16)
    hidden = lax.all_gather(hidden_share, ("dp", "guide"), axis=0, tiled=True)
    output_share = lax.psum_scatter(
        jnp.dot(hidden, w_down, preferred_element_type=F32), "mp", scatter_dimension=0, tiled=True)
    return output_share.astype(BF16)


def solution(mesh):
    line = mesh.shape["mp"] == 4 and mesh.shape["dp"] == 2 and mesh.shape["guide"] == 2

    def per_device(tokens, w_gate, w_up, w_down):
        rows, depth = tokens.shape
        columns, wide = w_gate.shape[1], w_down.shape[1]
        whole = (rows % 8 == 0 and depth % (128 * PIECES) == 0 and columns % 512 == 0 and columns >= 2048
                 and wide % (128 * N_OUT) == 0)
        if line and whole:
            return fused(tokens, w_gate, w_up, w_down)
        return by_collectives(tokens, w_gate, w_up, w_down)

    placed = (
        P(("groups", "mp"), ("dp", "guide")),
        P(("dp", "guide"), "mp"),
        P(("dp", "guide"), "mp"),
        P("mp", ("dp", "guide")),
    )
    return jax.shard_map(
        per_device, mesh=mesh, in_specs=placed,
        out_specs=P(("groups", "mp"), ("dp", "guide")), check_vma=False)
```

```python
import functools

import jax
import jax.numpy as jnp
from jax import lax
from jax.experimental import pallas as pl
from jax.experimental.pallas import tpu as pltpu
from jax.sharding import PartitionSpec as P

MESH = pl.DeviceIdType.MESH
F32, BF16 = jnp.float32, jnp.bfloat16
PIECES = 4
K_GROUPS = ((0, 2), (2, 3), (3, 4))
N_OUT = 4


def splits(width, most):
    cuts = list(range(0, width, most)) + [width]
    return tuple((lo, hi - lo) for lo, hi in zip(cuts, cuts[1:]))


BLOCKS = ((0, 1), (1, 2), (2, 4))


def kernel(tokens, w_gate, w_up, w_down, out, *scratch):
    (pair_v, down_v, tok_in, tok_f, tok, lhs, acc, out_send, part_recv, out_recv,
     w_sem, down_sem, tok_own, tok_s, near_r, far_r, c_s, part_r, sum_r, c_r) = scratch[:20]
    (sum1_out, sum1_in, kept, sum2_out, sum2_in, hid,
     s1_s, s1_r, s2_s, s2_r, hx_s, hx_r, hc_s, hc_r, hr_s, hr_r) = [
        [scratch[20 + 16 * b + i] for b in range(len(BLOCKS))] for i in range(16)]
    m, d, g = lax.axis_index("mp"), lax.axis_index("dp"), lax.axis_index("guide")
    rows, depth = tokens.shape
    quarter = pair_v.shape[2] // 2
    wide = down_v.shape[1]
    cols = chunks(quarter)
    nc = len(cols)
    piece = depth // PIECES
    n_width = wide // N_OUT
    z1 = m + 1 - 2 * lax.rem(m, 2)
    z2 = lax.rem(m + 2, 4)
    z3 = 3 - m
    mid = lax.rem(m + 1, 4) // 2
    to_dp, to_core = {"dp": 1 - d}, {"guide": 1 - g}

    barrier = pltpu.get_barrier_semaphore()
    for device in ({"mp": z1}, {"mp": z2}, {"mp": z3}, to_dp, to_core):
        pl.semaphore_signal(barrier, inc=1, device_id=device, device_id_type=MESH)

    def region(dd, gg):
        return pl.multiple_of((gg * 2 + dd) * quarter, 128)

    regions = (region(1 - d, 1 - g), region(1 - d, g), region(d, 1 - g), region(d, g))
    hid_regions = (region(d, g), region(d, 1 - g), region(1 - d, g), region(1 - d, 1 - g))

    def weights(s):
        src = pl.ds(regions[s], quarter)
        return [pltpu.make_async_copy(w.at[:, src], pair_v.at[s, :, pl.ds(i * quarter, quarter)], w_sem.at[s])
                for i, w in ((0, w_gate), (1, w_up))]

    def weights_wait(s):
        pltpu.make_async_copy(pair_v.at[s], pair_v.at[s], w_sem.at[s]).wait()

    def downs(s):
        return pltpu.make_async_copy(
            w_down.at[pl.ds(hid_regions[s], quarter), :], down_v.at[pl.ds(s * quarter, quarter), :], down_sem.at[s // 2])

    def downs_wait(half):
        part = down_v.at[pl.ds(half * 2 * quarter, 2 * quarter), :]
        pltpu.make_async_copy(part, part, down_sem.at[half]).wait()

    own = pltpu.make_async_copy(tokens, tok_in.at[3], tok_own)
    own.start()
    own.wait()
    for s in range(4):
        for copy in weights(s):
            copy.start()
    for s in range(4):
        downs(s).start()

    pl.semaphore_wait(barrier, 5)

    tok_z1 = pltpu.make_async_remote_copy(
        src_ref=tok_in.at[3], dst_ref=tok_in.at[2], send_sem=tok_s.at[2], recv_sem=near_r,
        device_id={"mp": z1}, device_id_type=MESH)

    def tok_copy(p, kind, src, to):
        c = pl.ds(p * piece, piece)
        return pltpu.make_async_remote_copy(
            src_ref=tok_in.at[src, :, c], dst_ref=tok_in.at[mid, :, c], send_sem=tok_s.at[kind], recv_sem=far_r.at[kind, p],
            device_id={"mp": to}, device_id_type=MESH)

    def tok_z3(p):
        return tok_copy(p, 0, 3, z3)

    def tok_z2(p):
        return tok_copy(p, 1, 3, z2)

    def tok_relay(p):
        return tok_copy(p, 1, 1, z1)

    @pl.when(mid == 1)
    def _():
        for p in range(PIECES // 2):
            tok_z3(p).start()
        tok_z1.start()
        for p in range(PIECES // 2, PIECES):
            tok_z3(p).start()

    @pl.when(mid == 0)
    def _():
        tok_z1.start()
        for p in range(PIECES):
            tok_z3(p).start()
            tok_z2(p).start()

    def forward(p):
        @pl.when(mid == 1)
        def _():
            tok_z3(p).wait_recv()
            tok_relay(p).start()

    def gather_far(p):
        @pl.when(mid == 0)
        def _():
            tok_z3(p).wait_recv()

        tok_z2(p).wait_recv()
        c = slice(p * piece, (p + 1) * piece)
        for q in range(2):
            tok_f[q * rows:(q + 1) * rows, c] = tok_in[q, :, c].astype(F32)
        tok[:2 * rows, c] = tok_f[:, c].astype(BF16)

    def gather_near():
        tok_z1.wait_recv()
        for q in range(2):
            tok_f[q * rows:(q + 1) * rows, :] = tok_in[2 + q].astype(F32)
        tok[2 * rows:, :] = tok_f[...].astype(BF16)

    def add_up(s, k, first, blocks):
        to = sum1_out if s % 2 == 0 else kept
        base, end = BLOCKS[blocks[0]][0], BLOCKS[blocks[-1]][1]
        value = jnp.dot(tok[base * rows:end * rows, k], pair_v[s, k, :], preferred_element_type=F32)
        for i in range(2):
            for b in blocks:
                lo, hi = BLOCKS[b][0] - base, BLOCKS[b][1] - base
                part = value[lo * rows:hi * rows, i * quarter:(i + 1) * quarter]
                if first:
                    to[b][s // 2, i] = part
                else:
                    to[b][s // 2, i] += part

    def partial_near(s):
        weights_wait(s)
        add_up(s, slice(0, depth), True, (2,))

    def partial_far(kg, s):
        add_up(s, slice(K_GROUPS[kg][0] * piece, K_GROUPS[kg][1] * piece), kg == 0, (0, 1))

    def partial_all(s):
        weights_wait(s)
        add_up(s, slice(0, depth), True, (0, 1, 2))

    def s1_copy(i, b):
        return pltpu.make_async_remote_copy(
            src_ref=sum1_out[b].at[i], dst_ref=sum1_in[b].at[i], send_sem=s1_s[b], recv_sem=s1_r[b].at[i],
            device_id=to_core, device_id_type=MESH)

    def send_core(i, *blocks):
        for b in blocks:
            s1_copy(i, b).start()

    def s2_copy(b, start, width, recv):
        part = pl.ds(start, width)
        return pltpu.make_async_remote_copy(
            src_ref=sum2_out[b].at[:, :, part], dst_ref=sum2_in[b].at[:, :, part],
            send_sem=s2_s[b], recv_sem=recv, device_id=to_dp, device_id_type=MESH)

    def pair_sum(b):
        s1_copy(0, b).wait_recv()
        for c, (start, width) in enumerate(cols):
            part = slice(start, start + width)
            for i in range(2):
                sum2_out[b][i, :, part] = (kept[b][0, i, :, part] + sum1_in[b][0, i, :, part]).astype(BF16)
            s2_copy(b, start, width, s2_r[b].at[c]).start()

    def hid_copy(b, start, width, src, dst, send, recv, to):
        return pltpu.make_async_remote_copy(
            src_ref=hid[b].at[:, pl.ds(src * quarter + start, width)],
            dst_ref=hid[b].at[:, pl.ds(dst * quarter + start, width)],
            send_sem=send, recv_sem=recv, device_id=to, device_id_type=MESH)

    def hx_copy(b, c):
        return hid_copy(b, *cols[c], 0, 2, hx_s[b], hx_r[b].at[c], to_dp)

    def hc_copy(b, start, width):
        return hid_copy(b, start, width, 0, 1, hc_s[b], hc_r[b], to_core)

    def hr_copy(b, start, width):
        return hid_copy(b, start, width, 2, 3, hr_s[b], hr_r[b], to_core)

    def finish(b, c):
        if c == 0:
            s1_copy(1, b).wait_recv()
        start, width = cols[c]
        part = slice(start, start + width)
        s2_copy(b, start, width, s2_r[b].at[c]).wait_recv()
        gate, up = [kept[b][1, i, :, part] + sum1_in[b][1, i, :, part] + sum2_in[b][i, :, part].astype(F32)
                    for i in range(2)]
        hid[b][:, part] = (gate / (1.0 + jnp.exp(-gate)) * up).astype(BF16)

    def send_x(b, c):
        hx_copy(b, c).start()

    def send_c(b, c):
        hc_copy(b, *cols[c]).start()

    def relay(b, c):
        hx_copy(b, c).wait_recv()
        hr_copy(b, *cols[c]).start()

    def part_copy(n, b):
        return pltpu.make_async_remote_copy(
            src_ref=out_send.at[b, n], dst_ref=part_recv.at[b, n], send_sem=c_s.at[b], recv_sem=part_r.at[b, n],
            device_id={"mp": z1}, device_id_type=MESH)

    def sum_copy(n, b):
        return pltpu.make_async_remote_copy(
            src_ref=out_send.at[b, n], dst_ref=out_recv.at[0, n], send_sem=c_s.at[b], recv_sem=sum_r.at[n],
            device_id={"mp": (z2, z3)[b]}, device_id_type=MESH)

    def near_copy(n):
        return pltpu.make_async_remote_copy(
            src_ref=out_send.at[2, n], dst_ref=out_recv.at[1, n], send_sem=c_s.at[2], recv_sem=c_r,
            device_id={"mp": z1}, device_id_type=MESH)

    def n_cols(n):
        return slice(n * n_width, (n + 1) * n_width)

    def down_first(*parts):
        if parts[0] == 0:
            downs_wait(0)
            for b in range(len(BLOCKS)):
                hc_copy(b, 0, quarter).wait_recv()
            part = slice(0, 2 * quarter)
            lhs[...] = jnp.concatenate([hid[b][:, part].astype(F32) for b in range(3)], axis=0).astype(BF16)
        for n in parts:
            acc[:, n_cols(n)] = jnp.dot(lhs[...], down_v[:2 * quarter, n_cols(n)], preferred_element_type=F32)

    def far_out(n, b):
        @pl.when(mid == 0)
        def _():
            out_send[b, n] = acc[b * rows:(b + 1) * rows, n_cols(n)].astype(BF16)
            part_copy(n, b).start()

    def middle(b):
        @pl.when(mid == 1)
        def _():
            for n in range(N_OUT):
                part_copy(n, b).wait_recv()
                total = acc[b * rows:(b + 1) * rows, n_cols(n)] + part_recv[b, n].astype(F32)
                out_send[b, n] = total.astype(BF16)
                sum_copy(n, b).start()

    def down_second(n):
        acc[:rows, n_cols(n)] += jnp.dot(
            hid[0][:, 2 * quarter:], down_v[2 * quarter:, n_cols(n)], preferred_element_type=F32)

    def down_third(n):
        if n == 0:
            part = slice(2 * quarter, 4 * quarter)
            lhs[:3 * rows, :] = jnp.concatenate([hid[b][:, part].astype(F32) for b in (1, 2)], axis=0).astype(BF16)
        acc[rows:, n_cols(n)] += jnp.dot(
            lhs[:3 * rows, :], down_v[2 * quarter:, n_cols(n)], preferred_element_type=F32)

    def near_out(n):
        out_send[2, n] = acc[2 * rows:3 * rows, n_cols(n)].astype(BF16)
        near_copy(n).start()

    def final(n):
        sum_copy(n, 0).wait_recv()
        total = acc[3 * rows:, n_cols(n)] + out_recv[0, n].astype(F32) + out_recv[1, n].astype(F32)
        out[:, n_cols(n)] = total.astype(BF16)

    def s1_whole(b):
        return pltpu.make_async_remote_copy(
            src_ref=sum1_out[b], dst_ref=sum1_in[b], send_sem=s1_s[b], recv_sem=s1_r[b].at[0],
            device_id=to_core, device_id_type=MESH)

    def tok_far_whole(kind):
        return pltpu.make_async_remote_copy(
            src_ref=tok_in.at[3], dst_ref=tok_in.at[2], send_sem=tok_s.at[kind], recv_sem=near_r,
            device_id={"mp": z1}, device_id_type=MESH)

    def out_whole(b):
        return pltpu.make_async_remote_copy(
            src_ref=out_send.at[b], dst_ref=part_recv.at[0], send_sem=c_s.at[b], recv_sem=c_r,
            device_id={"mp": z1}, device_id_type=MESH)

    def near_whole():
        return pltpu.make_async_remote_copy(
            src_ref=out_send.at[2], dst_ref=out_recv.at[1], send_sem=c_s.at[2], recv_sem=c_r,
            device_id={"mp": z1}, device_id_type=MESH)

    forward(0)
    forward(1)
    forward(2)
    forward(3)
    gather_near()
    partial_near(0)
    send_core(0, 2)
    partial_near(1)
    pair_sum(2)
    gather_far(0)
    gather_far(1)
    partial_far(0, 0)
    partial_far(0, 1)
    gather_far(2)
    partial_far(1, 0)
    partial_far(1, 1)
    gather_far(3)
    partial_far(2, 0)
    send_core(0, 0, 1)
    partial_far(2, 1)
    pair_sum(0)
    pair_sum(1)
    partial_all(2)
    send_core(1, 0, 1, 2)
    partial_all(3)
    finish(2, 0)
    send_c(2, 0)
    finish(0, 0)
    send_x(0, 0)
    send_c(0, 0)
    finish(2, 1)
    send_c(2, 1)
    finish(0, 1)
    send_x(0, 1)
    send_c(0, 1)
    send_x(2, 0)
    finish(1, 0)
    send_x(1, 0)
    send_c(1, 0)
    finish(1, 1)
    send_x(1, 1)
    send_c(1, 1)
    send_x(2, 1)
    down_first(0, 1)
    relay(0, 0)
    relay(0, 1)
    down_first(2, 3)
    downs_wait(1)
    hr_copy(0, 0, quarter).wait_recv()
    down_second(0)
    down_second(1)
    far_out(0, 0)
    down_second(2)
    far_out(1, 0)
    relay(2, 0)
    relay(1, 0)
    relay(1, 1)
    relay(2, 1)
    down_second(3)
    far_out(2, 0)
    far_out(3, 0)
    hr_copy(1, 0, quarter).wait_recv()
    hr_copy(2, 0, quarter).wait_recv()
    down_third(0)
    down_third(1)
    far_out(0, 1)
    near_out(0)
    down_third(2)
    far_out(1, 1)
    near_out(1)
    down_third(3)
    far_out(2, 1)
    near_out(2)
    far_out(3, 1)
    near_out(3)
    middle(0)
    middle(1)
    for b in range(len(BLOCKS)):
        s1_whole(b).wait_send()
        s2_copy(b, 0, quarter, s2_r[b].at[0]).wait_send()
        hid_copy(b, 0, quarter, 0, 2, hx_s[b], hx_r[b].at[0], to_dp).wait_send()
        hc_copy(b, 0, quarter).wait_send()
        hr_copy(b, 0, quarter).wait_send()
    tok_z1.wait_send()
    for kind in range(2):
        tok_far_whole(kind).wait_send()
    near_whole().wait_recv()
    final(0)
    final(1)
    final(2)
    final(3)
    for b in range(3):
        out_whole(b).wait_send()


def chunks(quarter):
    return splits(quarter, (quarter // 128 + 1) // 2 * 128)


def fused(tokens, w_gate, w_up, w_down):
    rows, depth = tokens.shape
    columns, wide = w_gate.shape[1], w_down.shape[1]
    quarter = columns // 4
    nc, n_width = len(chunks(quarter)), wide // N_OUT
    dma, vmem = pltpu.SemaphoreType.DMA, pltpu.VMEM
    shapes = [
        vmem((4, depth, 2 * quarter), BF16),
        vmem((columns, wide), BF16),
        vmem((4, rows, depth), BF16),
        vmem((2 * rows, depth), F32),
        vmem((4 * rows, depth), BF16),
        vmem((4 * rows, 2 * quarter), BF16),
        vmem((4 * rows, wide), F32),
        vmem((3, N_OUT, rows, n_width), BF16),
        vmem((2, N_OUT, rows, n_width), BF16),
        vmem((2, N_OUT, rows, n_width), BF16),
        dma((4,)), dma((2,)), dma, dma((3,)), dma, dma((2, PIECES)),
        dma((3,)), dma((2, N_OUT)), dma((N_OUT,)), dma,
    ]
    for lo, hi in BLOCKS:
        size = (hi - lo) * rows
        shapes += [vmem((2, 2, size, quarter), F32)] * 3 + [vmem((2, size, quarter), BF16)] * 2
        shapes += [vmem((size, columns), BF16)]
        shapes += [dma, dma((2,)), dma, dma((nc,)), dma, dma((nc,)), dma, dma, dma, dma]
    return pl.pallas_call(
        kernel,
        out_shape=vmem((rows, wide), BF16),
        in_specs=[pl.BlockSpec(memory_space=pltpu.HBM)] * 4,
        out_specs=pl.BlockSpec(memory_space=vmem),
        scratch_shapes=shapes,
        compiler_params=pltpu.CompilerParams(
            collective_id=0, has_side_effects=True, vmem_limit_bytes=60 << 20),
    )(tokens, w_gate, w_up, w_down)


def by_collectives(tokens, w_gate, w_up, w_down):
    columns = w_gate.shape[1]
    paired_weights = jnp.concatenate([w_gate, w_up], axis=1)
    partial_terms = jnp.dot(
        lax.all_gather(tokens, "mp", axis=0, tiled=True), paired_weights, preferred_element_type=F32)
    summed = lax.psum_scatter(partial_terms, ("dp", "guide"), scatter_dimension=0, tiled=True)
    hidden_share = (jax.nn.silu(summed[:, :columns]) * summed[:, columns:]).astype(BF16)
    hidden = lax.all_gather(hidden_share, ("dp", "guide"), axis=0, tiled=True)
    output_share = lax.psum_scatter(
        jnp.dot(hidden, w_down, preferred_element_type=F32), "mp", scatter_dimension=0, tiled=True)
    return output_share.astype(BF16)


def solution(mesh):
    line = mesh.shape["mp"] == 4 and mesh.shape["dp"] == 2 and mesh.shape["guide"] == 2

    def per_device(tokens, w_gate, w_up, w_down):
        rows, depth = tokens.shape
        columns, wide = w_gate.shape[1], w_down.shape[1]
        whole = (rows % 8 == 0 and depth % (128 * PIECES) == 0 and columns % 512 == 0 and columns >= 2048
                 and wide % (128 * N_OUT) == 0)
        if line and whole:
            return fused(tokens, w_gate, w_up, w_down)
        return by_collectives(tokens, w_gate, w_up, w_down)

    placed = (
        P(("groups", "mp"), ("dp", "guide")),
        P(("dp", "guide"), "mp"),
        P(("dp", "guide"), "mp"),
        P("mp", ("dp", "guide")),
    )
    return jax.shard_map(
        per_device, mesh=mesh, in_specs=placed,
        out_specs=P(("groups", "mp"), ("dp", "guide")), check_vma=False)
```

```python
import functools

import jax
import jax.numpy as jnp
from jax import lax
from jax.experimental import pallas as pl
from jax.experimental.pallas import tpu as pltpu
from jax.sharding import PartitionSpec as P

MESH = pl.DeviceIdType.MESH
F32, BF16 = jnp.float32, jnp.bfloat16
PIECES = 4
K_GROUPS = ((0, 2), (2, 4))
N_OUT = 4


def splits(width, most):
    cuts = list(range(0, width, most)) + [width]
    return tuple((lo, hi - lo) for lo, hi in zip(cuts, cuts[1:]))


BLOCKS = ((0, 1), (1, 2), (2, 4))


def kernel(tokens, w_gate, w_up, w_down, out, *scratch):
    (pair_v, down_v, tok_in, tok_f, tok, lhs, acc, out_send, part_recv, out_recv,
     w_sem, down_sem, tok_own, tok_s, near_r, far_r, c_s, part_r, sum_r, c_r) = scratch[:20]
    (sum1_out, sum1_in, kept, sum2_out, sum2_in, hid,
     s1_s, s1_r, s2_s, s2_r, hx_s, hx_r, hc_s, hc_r, hr_s, hr_r) = [
        [scratch[20 + 16 * b + i] for b in range(len(BLOCKS))] for i in range(16)]
    m, d, g = lax.axis_index("mp"), lax.axis_index("dp"), lax.axis_index("guide")
    rows, depth = tokens.shape
    quarter = pair_v.shape[2] // 2
    wide = down_v.shape[1]
    cols = chunks(quarter)
    nc = len(cols)
    piece = depth // PIECES
    n_width = wide // N_OUT
    z1 = m + 1 - 2 * lax.rem(m, 2)
    z2 = lax.rem(m + 2, 4)
    z3 = 3 - m
    mid = lax.rem(m + 1, 4) // 2
    to_dp, to_core = {"dp": 1 - d}, {"guide": 1 - g}

    barrier = pltpu.get_barrier_semaphore()
    for device in ({"mp": z1}, {"mp": z2}, {"mp": z3}, to_dp, to_core):
        pl.semaphore_signal(barrier, inc=1, device_id=device, device_id_type=MESH)

    def region(dd, gg):
        return pl.multiple_of((gg * 2 + dd) * quarter, 128)

    regions = (region(1 - d, 1 - g), region(1 - d, g), region(d, 1 - g), region(d, g))
    hid_regions = (region(d, g), region(d, 1 - g), region(1 - d, g), region(1 - d, 1 - g))

    def weights(s):
        src = pl.ds(regions[s], quarter)
        return [pltpu.make_async_copy(w.at[:, src], pair_v.at[s, :, pl.ds(i * quarter, quarter)], w_sem.at[s])
                for i, w in ((0, w_gate), (1, w_up))]

    def weights_wait(s):
        pltpu.make_async_copy(pair_v.at[s], pair_v.at[s], w_sem.at[s]).wait()

    def downs(s):
        return pltpu.make_async_copy(
            w_down.at[pl.ds(hid_regions[s], quarter), :], down_v.at[pl.ds(s * quarter, quarter), :], down_sem.at[s // 2])

    def downs_wait(half):
        part = down_v.at[pl.ds(half * 2 * quarter, 2 * quarter), :]
        pltpu.make_async_copy(part, part, down_sem.at[half]).wait()

    own = pltpu.make_async_copy(tokens, tok_in.at[3], tok_own)
    own.start()
    own.wait()
    for s in range(4):
        for copy in weights(s):
            copy.start()
    for s in range(4):
        downs(s).start()

    pl.semaphore_wait(barrier, 5)

    tok_z1 = pltpu.make_async_remote_copy(
        src_ref=tok_in.at[3], dst_ref=tok_in.at[2], send_sem=tok_s.at[2], recv_sem=near_r,
        device_id={"mp": z1}, device_id_type=MESH)

    def tok_copy(p, kind, src, to):
        c = pl.ds(p * piece, piece)
        return pltpu.make_async_remote_copy(
            src_ref=tok_in.at[src, :, c], dst_ref=tok_in.at[mid, :, c], send_sem=tok_s.at[kind], recv_sem=far_r.at[kind, p],
            device_id={"mp": to}, device_id_type=MESH)

    def tok_z3(p):
        return tok_copy(p, 0, 3, z3)

    def tok_z2(p):
        return tok_copy(p, 1, 3, z2)

    def tok_relay(p):
        return tok_copy(p, 1, 1, z1)

    @pl.when(mid == 1)
    def _():
        tok_z1.start()
        for p in range(PIECES):
            tok_z3(p).start()

    @pl.when(mid == 0)
    def _():
        tok_z1.start()
        for p in range(PIECES):
            tok_z3(p).start()
            tok_z2(p).start()

    def forward(p):
        @pl.when(mid == 1)
        def _():
            tok_z3(p).wait_recv()
            tok_relay(p).start()

    def gather_far(p):
        @pl.when(mid == 0)
        def _():
            tok_z3(p).wait_recv()

        tok_z2(p).wait_recv()
        c = slice(p * piece, (p + 1) * piece)
        for q in range(2):
            tok_f[q * rows:(q + 1) * rows, c] = tok_in[q, :, c].astype(F32)
        tok[:2 * rows, c] = tok_f[:, c].astype(BF16)

    def gather_near():
        tok_z1.wait_recv()
        for q in range(2):
            tok_f[q * rows:(q + 1) * rows, :] = tok_in[2 + q].astype(F32)
        tok[2 * rows:, :] = tok_f[...].astype(BF16)

    def add_up(s, k, first, blocks):
        to = sum1_out if s % 2 == 0 else kept
        base, end = BLOCKS[blocks[0]][0], BLOCKS[blocks[-1]][1]
        left = tok[base * rows:end * rows, k]
        for i in range(2):
            for start, width in splits(quarter, 512):
                at = i * quarter + start
                value = jnp.dot(left, pair_v[s, k, at:at + width], preferred_element_type=F32)
                for b in blocks:
                    lo, hi = BLOCKS[b][0] - base, BLOCKS[b][1] - base
                    part = value[lo * rows:hi * rows, :]
                    if first:
                        to[b][s // 2, i, :, start:start + width] = part
                    else:
                        to[b][s // 2, i, :, start:start + width] += part

    def partial_near(s):
        weights_wait(s)
        add_up(s, slice(0, depth), True, (2,))

    def partial_far(kg, s):
        add_up(s, slice(K_GROUPS[kg][0] * piece, K_GROUPS[kg][1] * piece), kg == 0, (0, 1))

    def partial_far_whole(s):
        add_up(s, slice(0, depth), True, (0, 1))

    def partial_all(s):
        weights_wait(s)
        add_up(s, slice(0, depth), True, (0, 1, 2))

    def s1_copy(i, b):
        return pltpu.make_async_remote_copy(
            src_ref=sum1_out[b].at[i], dst_ref=sum1_in[b].at[i], send_sem=s1_s[b], recv_sem=s1_r[b].at[i],
            device_id=to_core, device_id_type=MESH)

    def send_core(i, *blocks):
        for b in blocks:
            s1_copy(i, b).start()

    def s2_copy(b, start, width, recv):
        part = pl.ds(start, width)
        return pltpu.make_async_remote_copy(
            src_ref=sum2_out[b].at[:, :, part], dst_ref=sum2_in[b].at[:, :, part],
            send_sem=s2_s[b], recv_sem=recv, device_id=to_dp, device_id_type=MESH)

    def pair_sum(b, c):
        if c == 0:
            s1_copy(0, b).wait_recv()
        start, width = cols[c]
        part = slice(start, start + width)
        for i in range(2):
            sum2_out[b][i, :, part] = (kept[b][0, i, :, part] + sum1_in[b][0, i, :, part]).astype(BF16)
        s2_copy(b, start, width, s2_r[b].at[c]).start()

    def hid_copy(b, start, width, src, dst, send, recv, to):
        return pltpu.make_async_remote_copy(
            src_ref=hid[b].at[:, pl.ds(src * quarter + start, width)],
            dst_ref=hid[b].at[:, pl.ds(dst * quarter + start, width)],
            send_sem=send, recv_sem=recv, device_id=to, device_id_type=MESH)

    def hx_copy(b, c):
        return hid_copy(b, *cols[c], 0, 2, hx_s[b], hx_r[b].at[c], to_dp)

    def hc_copy(b, start, width):
        return hid_copy(b, start, width, 0, 1, hc_s[b], hc_r[b], to_core)

    def hr_copy(b, start, width):
        return hid_copy(b, start, width, 2, 3, hr_s[b], hr_r[b], to_core)

    def finish(b, c):
        if c == 0:
            s1_copy(1, b).wait_recv()
        start, width = cols[c]
        part = slice(start, start + width)
        s2_copy(b, start, width, s2_r[b].at[c]).wait_recv()
        gate, up = [kept[b][1, i, :, part] + sum1_in[b][1, i, :, part] + sum2_in[b][i, :, part].astype(F32)
                    for i in range(2)]
        hid[b][:, part] = (gate / (1.0 + jnp.exp(-gate)) * up).astype(BF16)

    def send_x(b, c):
        hx_copy(b, c).start()

    def send_c(b, c):
        hc_copy(b, *cols[c]).start()

    def relay(b, c):
        hx_copy(b, c).wait_recv()
        hr_copy(b, *cols[c]).start()

    def part_copy(n, b):
        return pltpu.make_async_remote_copy(
            src_ref=out_send.at[b, n], dst_ref=part_recv.at[b, n], send_sem=c_s.at[b], recv_sem=part_r.at[b, n],
            device_id={"mp": z1}, device_id_type=MESH)

    def sum_copy(n, b):
        return pltpu.make_async_remote_copy(
            src_ref=out_send.at[b, n], dst_ref=out_recv.at[0, n], send_sem=c_s.at[b], recv_sem=sum_r.at[n],
            device_id={"mp": (z2, z3)[b]}, device_id_type=MESH)

    def near_copy(n):
        return pltpu.make_async_remote_copy(
            src_ref=out_send.at[2, n], dst_ref=out_recv.at[1, n], send_sem=c_s.at[2], recv_sem=c_r,
            device_id={"mp": z1}, device_id_type=MESH)

    def n_cols(n):
        return slice(n * n_width, (n + 1) * n_width)

    def far_out(n, b):
        out_send[b, n] = acc[b * rows:(b + 1) * rows, n_cols(n)].astype(BF16)
        part_copy(n, b).start()

    def middle(n, b):
        part_copy(n, b).wait_recv()
        total = acc[b * rows:(b + 1) * rows, n_cols(n)] + part_recv[b, n].astype(F32)
        out_send[b, n] = total.astype(BF16)
        sum_copy(n, b).start()

    def take(half, *blocks):
        for b in blocks:
            (hr_copy if half else hc_copy)(b, 0, quarter).wait_recv()
        if len(blocks) > 1:
            part = slice(half * 2 * quarter, (half + 1) * 2 * quarter)
            lhs[:rows_of(*blocks), :] = jnp.concatenate(
                [hid[b][:, part].astype(F32) for b in blocks], axis=0).astype(BF16)

    def rows_of(*blocks):
        return sum(BLOCKS[b][1] - BLOCKS[b][0] for b in blocks) * rows

    def down(n, half, *blocks):
        k = slice(half * 2 * quarter, (half + 1) * 2 * quarter)
        left = hid[blocks[0]][:, k] if len(blocks) == 1 else lhs[:rows_of(*blocks), :]
        value = jnp.dot(left, down_v[k, n_cols(n)], preferred_element_type=F32)
        for i, b in enumerate(blocks):
            lo, hi = rows_of(*blocks[:i]), rows_of(*blocks[:i + 1])
            at = slice(BLOCKS[b][0] * rows, BLOCKS[b][1] * rows)
            if half:
                acc[at, n_cols(n)] += value[lo:hi, :]
            else:
                acc[at, n_cols(n)] = value[lo:hi, :]

    def near_out(n):
        out_send[2, n] = acc[2 * rows:3 * rows, n_cols(n)].astype(BF16)
        near_copy(n).start()

    def hidden(b, c, x=True):
        finish(b, c)
        if x:
            send_x(b, c)
        send_c(b, c)

    def final(n):
        sum_copy(n, 0).wait_recv()
        total = acc[3 * rows:, n_cols(n)] + out_recv[0, n].astype(F32) + out_recv[1, n].astype(F32)
        out[:, n_cols(n)] = total.astype(BF16)

    def s1_whole(b):
        return pltpu.make_async_remote_copy(
            src_ref=sum1_out[b], dst_ref=sum1_in[b], send_sem=s1_s[b], recv_sem=s1_r[b].at[0],
            device_id=to_core, device_id_type=MESH)

    def tok_far_whole(kind):
        return pltpu.make_async_remote_copy(
            src_ref=tok_in.at[3], dst_ref=tok_in.at[2], send_sem=tok_s.at[kind], recv_sem=near_r,
            device_id={"mp": z1}, device_id_type=MESH)

    def out_whole(b):
        return pltpu.make_async_remote_copy(
            src_ref=out_send.at[b], dst_ref=part_recv.at[0], send_sem=c_s.at[b], recv_sem=c_r,
            device_id={"mp": z1}, device_id_type=MESH)

    def near_whole():
        return pltpu.make_async_remote_copy(
            src_ref=out_send.at[2], dst_ref=out_recv.at[1], send_sem=c_s.at[2], recv_sem=c_r,
            device_id={"mp": z1}, device_id_type=MESH)

    forward(0)
    forward(1)
    forward(2)
    forward(3)
    gather_near()
    partial_near(0)
    send_core(0, 2)
    partial_near(1)
    pair_sum(2, 0)

    @pl.when(mid == 1)
    def _():
        pair_sum(2, 1)

    gather_far(0)
    gather_far(1)
    partial_far(0, 0)
    gather_far(2)
    gather_far(3)
    partial_far(1, 0)
    send_core(0, 0, 1)
    partial_far_whole(1)
    pair_sum(0, 0)
    pair_sum(0, 1)
    pair_sum(1, 0)
    pair_sum(1, 1)

    partial_all(2)
    send_core(1, 0, 1, 2)
    partial_all(3)
    downs_wait(0)
    downs_wait(1)

    @pl.when(mid == 0)
    def _():
        hidden(2, 0, False)
        hidden(0, 0)
        hidden(0, 1)
        pair_sum(2, 1)
        hidden(1, 0)
        hidden(1, 1)
        send_x(2, 0)
        take(0, 0, 1)
        down(0, 0, 0, 1)
        relay(0, 0)
        down(1, 0, 0, 1)
        relay(0, 1)
        down(2, 0, 0, 1)
        down(3, 0, 0, 1)
        take(1, 0)
        down(0, 1, 0)
        down(1, 1, 0)
        far_out(0, 0)
        hidden(2, 1)
        down(2, 1, 0)
        far_out(1, 0)
        relay(1, 0)
        relay(1, 1)
        down(3, 1, 0)
        far_out(2, 0)
        far_out(3, 0)
        take(0, 2)
        down(0, 0, 2)
        down(1, 0, 2)
        take(1, 1)
        down(0, 1, 1)
        down(1, 1, 1)
        far_out(0, 1)
        down(2, 1, 1)
        far_out(1, 1)
        relay(2, 0)
        relay(2, 1)
        down(3, 1, 1)
        far_out(2, 1)
        far_out(3, 1)
        down(2, 0, 2)
        down(3, 0, 2)
        take(1, 2)
        down(0, 1, 2)
        down(1, 1, 2)
        near_out(0)
        down(2, 1, 2)
        near_out(1)
        down(3, 1, 2)
        near_out(2)
        near_out(3)

    @pl.when(mid == 1)
    def _():
        hidden(2, 0)
        hidden(2, 1, False)
        hidden(0, 0)
        hidden(0, 1)
        send_x(2, 1)
        hidden(1, 0)
        hidden(1, 1)
        take(0, 0, 1, 2)
        down(0, 0, 0, 1, 2)
        down(1, 0, 0, 1, 2)
        down(2, 0, 0, 1, 2)
        relay(0, 0)
        down(3, 0, 0, 1, 2)
        relay(0, 1)
        relay(2, 0)
        relay(2, 1)
        take(1, 0, 2)
        down(0, 1, 0, 2)
        down(1, 1, 0, 2)
        near_out(0)
        relay(1, 0)
        relay(1, 1)
        down(2, 1, 0, 2)
        near_out(1)
        down(3, 1, 0, 2)
        near_out(2)
        near_out(3)
        take(1, 1)
        down(0, 1, 1)
        middle(0, 0)
        down(1, 1, 1)
        middle(1, 0)
        down(2, 1, 1)
        middle(2, 0)
        down(3, 1, 1)
        middle(3, 0)
        middle(0, 1)
        middle(1, 1)
        middle(2, 1)
        middle(3, 1)

    for b in range(len(BLOCKS)):
        s1_whole(b).wait_send()
        s2_copy(b, 0, quarter, s2_r[b].at[0]).wait_send()
        hid_copy(b, 0, quarter, 0, 2, hx_s[b], hx_r[b].at[0], to_dp).wait_send()
        hc_copy(b, 0, quarter).wait_send()
        hr_copy(b, 0, quarter).wait_send()
    tok_z1.wait_send()
    for kind in range(2):
        tok_far_whole(kind).wait_send()
    near_whole().wait_recv()
    final(0)
    final(1)
    final(2)
    final(3)
    for b in range(3):
        out_whole(b).wait_send()


def chunks(quarter):
    return splits(quarter, (quarter // 128 + 1) // 2 * 128)


def fused(tokens, w_gate, w_up, w_down):
    rows, depth = tokens.shape
    columns, wide = w_gate.shape[1], w_down.shape[1]
    quarter = columns // 4
    nc, n_width = len(chunks(quarter)), wide // N_OUT
    dma, vmem = pltpu.SemaphoreType.DMA, pltpu.VMEM
    shapes = [
        vmem((4, depth, 2 * quarter), BF16),
        vmem((columns, wide), BF16),
        vmem((4, rows, depth), BF16),
        vmem((2 * rows, depth), F32),
        vmem((4 * rows, depth), BF16),
        vmem((4 * rows, 2 * quarter), BF16),
        vmem((4 * rows, wide), F32),
        vmem((3, N_OUT, rows, n_width), BF16),
        vmem((2, N_OUT, rows, n_width), BF16),
        vmem((2, N_OUT, rows, n_width), BF16),
        dma((4,)), dma((2,)), dma, dma((3,)), dma, dma((2, PIECES)),
        dma((3,)), dma((2, N_OUT)), dma((N_OUT,)), dma,
    ]
    for lo, hi in BLOCKS:
        size = (hi - lo) * rows
        shapes += [vmem((2, 2, size, quarter), F32)] * 3 + [vmem((2, size, quarter), BF16)] * 2
        shapes += [vmem((size, columns), BF16)]
        shapes += [dma, dma((2,)), dma, dma((nc,)), dma, dma((nc,)), dma, dma, dma, dma]
    return pl.pallas_call(
        kernel,
        out_shape=vmem((rows, wide), BF16),
        in_specs=[pl.BlockSpec(memory_space=pltpu.HBM)] * 4,
        out_specs=pl.BlockSpec(memory_space=vmem),
        scratch_shapes=shapes,
        compiler_params=pltpu.CompilerParams(
            collective_id=0, has_side_effects=True, vmem_limit_bytes=60 << 20),
    )(tokens, w_gate, w_up, w_down)


def by_collectives(tokens, w_gate, w_up, w_down):
    columns = w_gate.shape[1]
    paired_weights = jnp.concatenate([w_gate, w_up], axis=1)
    partial_terms = jnp.dot(
        lax.all_gather(tokens, "mp", axis=0, tiled=True), paired_weights, preferred_element_type=F32)
    summed = lax.psum_scatter(partial_terms, ("dp", "guide"), scatter_dimension=0, tiled=True)
    hidden_share = (jax.nn.silu(summed[:, :columns]) * summed[:, columns:]).astype(BF16)
    hidden = lax.all_gather(hidden_share, ("dp", "guide"), axis=0, tiled=True)
    output_share = lax.psum_scatter(
        jnp.dot(hidden, w_down, preferred_element_type=F32), "mp", scatter_dimension=0, tiled=True)
    return output_share.astype(BF16)


def solution(mesh):
    line = mesh.shape["mp"] == 4 and mesh.shape["dp"] == 2 and mesh.shape["guide"] == 2

    def per_device(tokens, w_gate, w_up, w_down):
        rows, depth = tokens.shape
        columns, wide = w_gate.shape[1], w_down.shape[1]
        whole = (rows % 8 == 0 and depth % (128 * PIECES) == 0 and columns % 512 == 0 and columns >= 2048
                 and wide % (128 * N_OUT) == 0)
        if line and whole:
            return fused(tokens, w_gate, w_up, w_down)
        return by_collectives(tokens, w_gate, w_up, w_down)

    placed = (
        P(("groups", "mp"), ("dp", "guide")),
        P(("dp", "guide"), "mp"),
        P(("dp", "guide"), "mp"),
        P("mp", ("dp", "guide")),
    )
    return jax.shard_map(
        per_device, mesh=mesh, in_specs=placed,
        out_specs=P(("groups", "mp"), ("dp", "guide")), check_vma=False)
```

```python
import functools

import jax
import jax.numpy as jnp
from jax import lax
from jax.experimental import pallas as pl
from jax.experimental.pallas import tpu as pltpu
from jax.sharding import PartitionSpec as P

MESH = pl.DeviceIdType.MESH
F32, BF16 = jnp.float32, jnp.bfloat16
PIECES = 4
K_GROUPS = ((0, 2), (2, 4))
N_OUT = 4


def splits(width, most):
    cuts = list(range(0, width, most)) + [width]
    return tuple((lo, hi - lo) for lo, hi in zip(cuts, cuts[1:]))


BLOCKS = ((0, 1), (1, 2), (2, 4))


def kernel(tokens, w_gate, w_up, w_down, out, *scratch):
    (pair_v, down_v, tok_in, tok_f, tok, lhs, acc, out_send, part_recv, out_recv,
     w_sem, down_sem, tok_own, tok_s, near_r, far_r, c_s, part_r, sum_r, c_r) = scratch[:20]
    (sum1_out, sum1_in, kept, sum2_out, sum2_in, hid,
     s1_s, s1_r, s2_s, s2_r, hx_s, hx_r, hc_s, hc_r, hr_s, hr_r) = [
        [scratch[20 + 16 * b + i] for b in range(len(BLOCKS))] for i in range(16)]
    m, d, g = lax.axis_index("mp"), lax.axis_index("dp"), lax.axis_index("guide")
    rows, depth = tokens.shape
    quarter = pair_v.shape[2] // 2
    wide = down_v.shape[1]
    cols = [chunks(b, quarter) for b in range(len(BLOCKS))]
    piece = depth // PIECES
    n_width = wide // N_OUT
    z1 = m + 1 - 2 * lax.rem(m, 2)
    z2 = lax.rem(m + 2, 4)
    z3 = 3 - m
    mid = lax.rem(m + 1, 4) // 2
    to_dp, to_core, to_both = {"dp": 1 - d}, {"guide": 1 - g}, {"dp": 1 - d, "guide": 1 - g}

    barrier = pltpu.get_barrier_semaphore()
    for device in ({"mp": z1}, {"mp": z2}, {"mp": z3}, to_dp, to_core, to_both):
        pl.semaphore_signal(barrier, inc=1, device_id=device, device_id_type=MESH)

    def region(dd, gg):
        return pl.multiple_of((gg * 2 + dd) * quarter, 128)

    regions = (region(1 - d, 1 - g), region(1 - d, g), region(d, 1 - g), region(d, g))
    hid_regions = (region(d, g), region(d, 1 - g), region(1 - d, g), region(1 - d, 1 - g))

    def weights(s):
        src = pl.ds(regions[s], quarter)
        return [pltpu.make_async_copy(w.at[:, src], pair_v.at[s, :, pl.ds(i * quarter, quarter)], w_sem.at[s])
                for i, w in ((0, w_gate), (1, w_up))]

    def weights_wait(s):
        pltpu.make_async_copy(pair_v.at[s], pair_v.at[s], w_sem.at[s]).wait()

    def downs(s):
        return pltpu.make_async_copy(
            w_down.at[pl.ds(hid_regions[s], quarter), :], down_v.at[pl.ds(s * quarter, quarter), :], down_sem.at[s // 2])

    def downs_wait(half):
        part = down_v.at[pl.ds(half * 2 * quarter, 2 * quarter), :]
        pltpu.make_async_copy(part, part, down_sem.at[half]).wait()

    own = pltpu.make_async_copy(tokens, tok_in.at[3], tok_own)
    own.start()
    own.wait()
    for s in range(4):
        for copy in weights(s):
            copy.start()
    for s in range(4):
        downs(s).start()

    pl.semaphore_wait(barrier, 6)

    tok_z1 = pltpu.make_async_remote_copy(
        src_ref=tok_in.at[3], dst_ref=tok_in.at[2], send_sem=tok_s.at[2], recv_sem=near_r,
        device_id={"mp": z1}, device_id_type=MESH)

    def tok_copy(p, kind, src, to):
        c = pl.ds(p * piece, piece)
        return pltpu.make_async_remote_copy(
            src_ref=tok_in.at[src, :, c], dst_ref=tok_in.at[mid, :, c], send_sem=tok_s.at[kind], recv_sem=far_r.at[kind, p],
            device_id={"mp": to}, device_id_type=MESH)

    def tok_z3(p):
        return tok_copy(p, 0, 3, z3)

    def tok_z2(p):
        return tok_copy(p, 1, 3, z2)

    def tok_relay(p):
        return tok_copy(p, 1, 1, z1)

    @pl.when(mid == 1)
    def _():
        tok_z1.start()
        for p in range(PIECES):
            tok_z3(p).start()

    @pl.when(mid == 0)
    def _():
        tok_z1.start()
        for p in range(PIECES):
            tok_z3(p).start()
            tok_z2(p).start()

    def forward(p):
        @pl.when(mid == 1)
        def _():
            tok_z3(p).wait_recv()
            tok_relay(p).start()

    def gather_far(p):
        @pl.when(mid == 0)
        def _():
            tok_z3(p).wait_recv()

        tok_z2(p).wait_recv()
        c = slice(p * piece, (p + 1) * piece)
        for q in range(2):
            tok_f[q * rows:(q + 1) * rows, c] = tok_in[q, :, c].astype(F32)
        tok[:2 * rows, c] = tok_f[:, c].astype(BF16)

    def gather_near():
        tok_z1.wait_recv()
        for q in range(2):
            tok_f[q * rows:(q + 1) * rows, :] = tok_in[2 + q].astype(F32)
        tok[2 * rows:, :] = tok_f[...].astype(BF16)

    def add_up(s, k, first, blocks):
        to = sum1_out if s % 2 == 0 else kept
        base, end = BLOCKS[blocks[0]][0], BLOCKS[blocks[-1]][1]
        left = tok[base * rows:end * rows, k]
        for i in range(2):
            for start, width in splits(quarter, 512):
                at = i * quarter + start
                value = jnp.dot(left, pair_v[s, k, at:at + width], preferred_element_type=F32)
                for b in blocks:
                    lo, hi = BLOCKS[b][0] - base, BLOCKS[b][1] - base
                    part = value[lo * rows:hi * rows, :]
                    if first:
                        to[b][s // 2, i, :, start:start + width] = part
                    else:
                        to[b][s // 2, i, :, start:start + width] += part

    def partial_near(s):
        weights_wait(s)
        add_up(s, slice(0, depth), True, (2,))

    def partial_far(kg, s):
        add_up(s, slice(K_GROUPS[kg][0] * piece, K_GROUPS[kg][1] * piece), kg == 0, (0, 1))

    def partial_far_whole(s):
        add_up(s, slice(0, depth), True, (0, 1))

    def partial_all(s):
        weights_wait(s)
        add_up(s, slice(0, depth), True, (0, 1, 2))

    def s1_copy(i, b):
        return pltpu.make_async_remote_copy(
            src_ref=sum1_out[b].at[i], dst_ref=sum1_in[b].at[i], send_sem=s1_s[b], recv_sem=s1_r[b].at[i],
            device_id=to_core, device_id_type=MESH)

    def send_core(i, *blocks):
        for b in blocks:
            s1_copy(i, b).start()

    def s2_copy(b, start, width, recv):
        part = pl.ds(start, width)
        return pltpu.make_async_remote_copy(
            src_ref=sum2_out[b].at[:, :, part], dst_ref=sum2_in[b].at[:, :, part],
            send_sem=s2_s[b], recv_sem=recv, device_id=to_dp, device_id_type=MESH)

    def pair_sum(b, c):
        if c == 0:
            s1_copy(0, b).wait_recv()
        start, width = cols[b][c]
        part = slice(start, start + width)
        for i in range(2):
            sum2_out[b][i, :, part] = (kept[b][0, i, :, part] + sum1_in[b][0, i, :, part]).astype(BF16)
        s2_copy(b, start, width, s2_r[b].at[c]).start()

    def hid_copy(b, start, width, src, dst, send, recv, to):
        return pltpu.make_async_remote_copy(
            src_ref=hid[b].at[:, pl.ds(src * quarter + start, width)],
            dst_ref=hid[b].at[:, pl.ds(dst * quarter + start, width)],
            send_sem=send, recv_sem=recv, device_id=to, device_id_type=MESH)

    def hx_copy(b, c):
        return hid_copy(b, *cols[b][c], 0, 2, hx_s[b], hx_r[b].at[c], to_dp)

    def hc_copy(b, start, width):
        return hid_copy(b, start, width, 0, 1, hc_s[b], hc_r[b], to_core)

    def hr_copy(b, start, width):
        return hid_copy(b, start, width, 2, 3, hr_s[b], hr_r[b], to_core)

    def direct(b, c):
        hid_copy(b, *cols[b][c], 0, 3, hr_s[b], hr_r[b], to_both).start()

    def finish(b, c):
        if c == 0:
            s1_copy(1, b).wait_recv()
        start, width = cols[b][c]
        part = slice(start, start + width)
        s2_copy(b, start, width, s2_r[b].at[c]).wait_recv()
        gate, up = [kept[b][1, i, :, part] + sum1_in[b][1, i, :, part] + sum2_in[b][i, :, part].astype(F32)
                    for i in range(2)]
        hid[b][:, part] = (gate / (1.0 + jnp.exp(-gate)) * up).astype(BF16)

    def send_x(b, c):
        hx_copy(b, c).start()

    def send_c(b, c):
        hc_copy(b, *cols[b][c]).start()

    def arrived(b):
        for c in range(len(cols[b])):
            hx_copy(b, c).wait_recv()

    def relay(b, c):
        hx_copy(b, c).wait_recv()
        hr_copy(b, *cols[b][c]).start()

    def part_copy(n, b):
        return pltpu.make_async_remote_copy(
            src_ref=out_send.at[b, n], dst_ref=part_recv.at[b, n], send_sem=c_s.at[b], recv_sem=part_r.at[b, n],
            device_id={"mp": z1}, device_id_type=MESH)

    def sum_copy(n, b):
        return pltpu.make_async_remote_copy(
            src_ref=out_send.at[b, n], dst_ref=out_recv.at[0, n], send_sem=c_s.at[b], recv_sem=sum_r.at[n],
            device_id={"mp": (z2, z3)[b]}, device_id_type=MESH)

    def near_copy(n):
        return pltpu.make_async_remote_copy(
            src_ref=out_send.at[2, n], dst_ref=out_recv.at[1, n], send_sem=c_s.at[2], recv_sem=c_r,
            device_id={"mp": z1}, device_id_type=MESH)

    def n_cols(n):
        return slice(n * n_width, (n + 1) * n_width)

    def far_out(n, b):
        out_send[b, n] = acc[b * rows:(b + 1) * rows, n_cols(n)].astype(BF16)
        part_copy(n, b).start()

    def middle(n, b):
        part_copy(n, b).wait_recv()
        total = acc[b * rows:(b + 1) * rows, n_cols(n)] + part_recv[b, n].astype(F32)
        out_send[b, n] = total.astype(BF16)
        sum_copy(n, b).start()

    def take(half, *blocks):
        for b in blocks:
            (hr_copy if half else hc_copy)(b, 0, quarter).wait_recv()
        if len(blocks) > 1:
            part = slice(half * 2 * quarter, (half + 1) * 2 * quarter)
            lhs[:rows_of(*blocks), :] = jnp.concatenate(
                [hid[b][:, part].astype(F32) for b in blocks], axis=0).astype(BF16)

    def rows_of(*blocks):
        return sum(BLOCKS[b][1] - BLOCKS[b][0] for b in blocks) * rows

    def down(n, half, *blocks):
        k = slice(half * 2 * quarter, (half + 1) * 2 * quarter)
        left = hid[blocks[0]][:, k] if len(blocks) == 1 else lhs[:rows_of(*blocks), :]
        value = jnp.dot(left, down_v[k, n_cols(n)], preferred_element_type=F32)
        for i, b in enumerate(blocks):
            lo, hi = rows_of(*blocks[:i]), rows_of(*blocks[:i + 1])
            at = slice(BLOCKS[b][0] * rows, BLOCKS[b][1] * rows)
            if half:
                acc[at, n_cols(n)] += value[lo:hi, :]
            else:
                acc[at, n_cols(n)] = value[lo:hi, :]

    def near_out(n):
        out_send[2, n] = acc[2 * rows:3 * rows, n_cols(n)].astype(BF16)
        near_copy(n).start()

    def hidden(b, c, x=True):
        finish(b, c)
        if x:
            send_x(b, c)
        send_c(b, c)

    def final(n):
        sum_copy(n, 0).wait_recv()
        total = acc[3 * rows:, n_cols(n)] + out_recv[0, n].astype(F32) + out_recv[1, n].astype(F32)
        out[:, n_cols(n)] = total.astype(BF16)

    def s1_whole(b):
        return pltpu.make_async_remote_copy(
            src_ref=sum1_out[b], dst_ref=sum1_in[b], send_sem=s1_s[b], recv_sem=s1_r[b].at[0],
            device_id=to_core, device_id_type=MESH)

    def tok_far_whole(kind):
        return pltpu.make_async_remote_copy(
            src_ref=tok_in.at[3], dst_ref=tok_in.at[2], send_sem=tok_s.at[kind], recv_sem=near_r,
            device_id={"mp": z1}, device_id_type=MESH)

    def out_whole(b):
        return pltpu.make_async_remote_copy(
            src_ref=out_send.at[b], dst_ref=part_recv.at[0], send_sem=c_s.at[b], recv_sem=c_r,
            device_id={"mp": z1}, device_id_type=MESH)

    def near_whole():
        return pltpu.make_async_remote_copy(
            src_ref=out_send.at[2], dst_ref=out_recv.at[1], send_sem=c_s.at[2], recv_sem=c_r,
            device_id={"mp": z1}, device_id_type=MESH)

    forward(0)
    forward(1)
    forward(2)
    forward(3)
    gather_near()
    partial_near(0)
    send_core(0, 2)
    partial_near(1)
    pair_sum(2, 0)

    @pl.when(mid == 1)
    def _():
        pair_sum(2, 1)

    gather_far(0)
    gather_far(1)
    partial_far(0, 0)
    gather_far(2)
    gather_far(3)
    partial_far(1, 0)
    send_core(0, 0, 1)
    partial_far_whole(1)
    pair_sum(0, 0)
    pair_sum(0, 1)
    pair_sum(1, 0)
    pair_sum(1, 1)

    partial_all(2)
    send_core(1, 0, 1, 2)
    partial_all(3)
    downs_wait(0)
    downs_wait(1)

    @pl.when(mid == 0)
    def _():
        hidden(2, 0, False)
        hidden(0, 0)
        direct(0, 0)
        hidden(0, 1)
        direct(0, 1)
        pair_sum(2, 1)
        hidden(1, 0)
        hidden(1, 1)
        send_x(2, 0)
        take(0, 0, 1)
        down(0, 0, 0, 1)
        down(1, 0, 0, 1)
        down(2, 0, 0, 1)
        down(3, 0, 0, 1)
        arrived(0)
        take(1, 0)
        down(0, 1, 0)
        down(1, 1, 0)
        far_out(0, 0)
        hidden(2, 1)
        down(2, 1, 0)
        far_out(1, 0)
        relay(1, 0)
        relay(1, 1)
        down(3, 1, 0)
        far_out(2, 0)
        far_out(3, 0)
        take(0, 2)
        down(0, 0, 2)
        down(1, 0, 2)
        take(1, 1)
        down(0, 1, 1)
        down(1, 1, 1)
        far_out(0, 1)
        down(2, 1, 1)
        far_out(1, 1)
        relay(2, 0)
        relay(2, 1)
        down(3, 1, 1)
        far_out(2, 1)
        far_out(3, 1)
        down(2, 0, 2)
        down(3, 0, 2)
        take(1, 2)
        down(0, 1, 2)
        down(1, 1, 2)
        near_out(0)
        down(2, 1, 2)
        near_out(1)
        down(3, 1, 2)
        near_out(2)
        near_out(3)

    @pl.when(mid == 1)
    def _():
        hidden(2, 0)
        hidden(2, 1)
        hidden(0, 0)
        hidden(0, 1)
        hidden(1, 0)
        hidden(1, 1)
        take(0, 0, 1, 2)
        down(0, 0, 0, 1, 2)
        down(1, 0, 0, 1, 2)
        relay(2, 0)
        down(2, 0, 0, 1, 2)
        relay(2, 1)
        down(3, 0, 0, 1, 2)
        relay(0, 0)
        take(1, 2)
        down(0, 1, 2)
        relay(0, 1)
        down(1, 1, 2)
        near_out(0)
        down(2, 1, 2)
        near_out(1)
        down(3, 1, 2)
        near_out(2)
        near_out(3)
        relay(1, 0)
        relay(1, 1)
        take(1, 0)
        down(0, 1, 0)
        down(1, 1, 0)
        middle(0, 0)
        down(2, 1, 0)
        middle(1, 0)
        down(3, 1, 0)
        middle(2, 0)
        middle(3, 0)
        take(1, 1)
        down(0, 1, 1)
        down(1, 1, 1)
        middle(0, 1)
        down(2, 1, 1)
        middle(1, 1)
        down(3, 1, 1)
        middle(2, 1)
        middle(3, 1)

    for b in range(len(BLOCKS)):
        s1_whole(b).wait_send()
        s2_copy(b, 0, quarter, s2_r[b].at[0]).wait_send()
        hid_copy(b, 0, quarter, 0, 2, hx_s[b], hx_r[b].at[0], to_dp).wait_send()
        hc_copy(b, 0, quarter).wait_send()
        hr_copy(b, 0, quarter).wait_send()
    tok_z1.wait_send()
    for kind in range(2):
        tok_far_whole(kind).wait_send()
    near_whole().wait_recv()
    final(0)
    final(1)
    final(2)
    final(3)
    for b in range(3):
        out_whole(b).wait_send()


def chunks(b, quarter):
    lanes = quarter // 128
    return splits(quarter, (lanes - (lanes + 1) // 4 if b == 2 else (lanes + 1) // 2) * 128)


def fused(tokens, w_gate, w_up, w_down):
    rows, depth = tokens.shape
    columns, wide = w_gate.shape[1], w_down.shape[1]
    quarter = columns // 4
    n_width = wide // N_OUT
    dma, vmem = pltpu.SemaphoreType.DMA, pltpu.VMEM
    shapes = [
        vmem((4, depth, 2 * quarter), BF16),
        vmem((columns, wide), BF16),
        vmem((4, rows, depth), BF16),
        vmem((2 * rows, depth), F32),
        vmem((4 * rows, depth), BF16),
        vmem((4 * rows, 2 * quarter), BF16),
        vmem((4 * rows, wide), F32),
        vmem((3, N_OUT, rows, n_width), BF16),
        vmem((2, N_OUT, rows, n_width), BF16),
        vmem((2, N_OUT, rows, n_width), BF16),
        dma((4,)), dma((2,)), dma, dma((3,)), dma, dma((2, PIECES)),
        dma((3,)), dma((2, N_OUT)), dma((N_OUT,)), dma,
    ]
    for b, (lo, hi) in enumerate(BLOCKS):
        size, nc = (hi - lo) * rows, len(chunks(b, quarter))
        shapes += [vmem((2, 2, size, quarter), F32)] * 3 + [vmem((2, size, quarter), BF16)] * 2
        shapes += [vmem((size, columns), BF16)]
        shapes += [dma, dma((2,)), dma, dma((nc,)), dma, dma((nc,)), dma, dma, dma, dma]
    return pl.pallas_call(
        kernel,
        out_shape=vmem((rows, wide), BF16),
        in_specs=[pl.BlockSpec(memory_space=pltpu.HBM)] * 4,
        out_specs=pl.BlockSpec(memory_space=vmem),
        scratch_shapes=shapes,
        compiler_params=pltpu.CompilerParams(
            collective_id=0, has_side_effects=True, vmem_limit_bytes=60 << 20),
    )(tokens, w_gate, w_up, w_down)


def by_collectives(tokens, w_gate, w_up, w_down):
    columns = w_gate.shape[1]
    paired_weights = jnp.concatenate([w_gate, w_up], axis=1)
    partial_terms = jnp.dot(
        lax.all_gather(tokens, "mp", axis=0, tiled=True), paired_weights, preferred_element_type=F32)
    summed = lax.psum_scatter(partial_terms, ("dp", "guide"), scatter_dimension=0, tiled=True)
    hidden_share = (jax.nn.silu(summed[:, :columns]) * summed[:, columns:]).astype(BF16)
    hidden = lax.all_gather(hidden_share, ("dp", "guide"), axis=0, tiled=True)
    output_share = lax.psum_scatter(
        jnp.dot(hidden, w_down, preferred_element_type=F32), "mp", scatter_dimension=0, tiled=True)
    return output_share.astype(BF16)


def solution(mesh):
    line = mesh.shape["mp"] == 4 and mesh.shape["dp"] == 2 and mesh.shape["guide"] == 2

    def per_device(tokens, w_gate, w_up, w_down):
        rows, depth = tokens.shape
        columns, wide = w_gate.shape[1], w_down.shape[1]
        whole = (rows % 8 == 0 and depth % (128 * PIECES) == 0 and columns % 512 == 0 and columns >= 2048
                 and wide % (128 * N_OUT) == 0)
        if line and whole:
            return fused(tokens, w_gate, w_up, w_down)
        return by_collectives(tokens, w_gate, w_up, w_down)

    placed = (
        P(("groups", "mp"), ("dp", "guide")),
        P(("dp", "guide"), "mp"),
        P(("dp", "guide"), "mp"),
        P("mp", ("dp", "guide")),
    )
    return jax.shard_map(
        per_device, mesh=mesh, in_specs=placed,
        out_specs=P(("groups", "mp"), ("dp", "guide")), check_vma=False)
```
